128 devices in a mesh: tok: 8 (over z_hi, x), wid: 16 (over z_lo, y, core).
Axes of the slice: x: 4, y: 4, z: 4 (z_hi: 2, z_lo: 2; z = z_hi * 2 + z_lo), core: 2. Of those that a mesh axis runs over, the one named last changes fastest.
Arguments:
- resident_x: float32 [16384, 16384], P('tok', 'wid'), may hold values from -0.53033006 to 0.53033006
- resident_g: float32 [16384, 16384], P('tok', 'wid'), may hold values from -0.53033006 to 0.53033006
- query_x: float32 [1024, 16384], P('tok', 'wid'), may hold values from -0.53033006 to 0.53033006
- query_g: float32 [1024, 16384], P('tok', 'wid'), may hold values from -0.53033006 to 0.53033006
Outputs:
- kernel: float32 [16384, 1024], P(('tok', 'wid'))
The draws below stay inside these ranges and needn't reach their ends.
All inputs are finite; a program needn't handle non-finite values.
Results may differ from the reference program's by a relative error of at most 0.0002.
Values sent between devices are 32-bit elements; how exact they have to be, the bound alone decides.
A program may use at most 128 MiB of HBM per device.

```python
import jax
import jax.numpy as jnp
from jax import lax

D = 16384
RESIDENT = 16384
QUERIES = 1024


def spiked(drawn, rng, source, target, parts, factor):
    def block_of(position):
        return (jnp.arange(drawn.shape[position]) // (drawn.shape[position] // parts)).reshape((-1,) + (1,) * (drawn.ndim - 1 - position))

    first = jax.random.permutation(rng, parts)[block_of(target)]
    second = (block_of(target) + parts // 2) % parts
    return jnp.where((block_of(source) == first) | (block_of(source) == second), factor * drawn, drawn)


def block_scale(own_key, extent, split, smallest, high):
    def one(axis_at, blocks):
        draws = jax.random.uniform(jax.random.fold_in(jax.random.fold_in(own_key, 6), axis_at), (blocks,), jnp.float32, smallest / len(split), high / len(split))
        return jnp.repeat(jnp.exp(draws), extent[axis_at] // blocks).reshape((-1,) + (1,) * (len(extent) - axis_at - 1))

    factor_of = one(*split[0])
    for cut in split[1:]:
        factor_of = factor_of * one(*cut)
    return factor_of


def gaussian(stream_key, shape, spread, most, cuts=(), kind=jnp.bfloat16):
    entries = spread * jax.random.normal(stream_key, shape, jnp.float32)
    if cuts:
        entries = entries * block_scale(stream_key, shape, cuts, -0.22, 0.18)
    return jnp.clip(entries, -most, most).astype(kind)


def heavy_noise(rng, extent, spread, bound, cuts, heavy, held_as=jnp.bfloat16):
    array = spread * jax.random.normal(rng, extent, jnp.float32)
    if cuts:
        array = array * block_scale(rng, extent, cuts, -0.22, 0.18)
    return jnp.clip(spiked(array, jax.random.fold_in(rng, 3), *heavy), -bound, bound).astype(held_as)


def setup_inputs(seed: int = 0) -> dict:
    key_list = jax.random.split(jax.random.key(seed), 5)
    resident_x = heavy_noise(key_list[0], (RESIDENT, D), (D ** -0.25), 0.53033006, ((0, 8), (1, 16)), (1, 0, 16, 2.0), jnp.float32)
    resident_g = gaussian(key_list[1], (RESIDENT, D), (D ** -0.25), 0.53033006, ((0, 8), (1, 16)), jnp.float32)
    query_x = gaussian(key_list[2], (QUERIES, D), (D ** -0.25), 0.53033006, ((0, 8), (1, 16)), jnp.float32)
    query_g = gaussian(key_list[3], (QUERIES, D), (D ** -0.25), 0.53033006, ((0, 8), (1, 16)), jnp.float32)
    return dict(resident_x=resident_x, resident_g=resident_g, query_x=query_x, query_g=query_g)


def inner(left, right):
    return lax.dot_general(left, right, (((1,), (1,)), ((), ())), precision=lax.Precision.HIGHEST, preferred_element_type=jnp.float32)


def reference(resident_x, resident_g, query_x, query_g):
    input_gram = inner(resident_x, query_x)
    grad_gram = inner(resident_g, query_g)
    return input_gram * grad_gram
```

```python
import functools

import jax
import jax.numpy as jnp
from jax import lax
from jax.experimental import pallas as pl
from jax.experimental.pallas import tpu as pltpu
from jax.sharding import PartitionSpec as P

MESH = pl.DeviceIdType.MESH
F32, BF16 = jnp.float32, jnp.bfloat16
NT = (((1,), (1,)), ((), ()))

BLOCKS = ((0, 1, 0, 0), (2, 5, 0, 1), (3, 6, 3, 0), (4, 7, 1, 0), (10, 11, 2, 0), (8, 12, 3, 1), (9, 13, 1, 1), (14, 15, 2, 1))
HALVED = (10, 11, 14, 15)
UNITS = 16
REL = (2, 1, 3, 0)
STAGES = 4


def kernel(rx, rg, qx, qg, out, rh, rl, qbuf, qcat, stage, pbuf, csum, y1, y2, zin,
           load_sem, stage_sem, ag_send, ag_recv, c_send, c_recv, y1_send, y1_recv, y2_send, y2_recv, z_send, z_recv):
    t, w = lax.axis_index("tok"), lax.axis_index("wid")
    zh, x = t // 4, t % 4
    zl, y, c = w // 8, (w // 2) % 4, w % 2
    right, left = (zh * 4 + (x + 1) % 4, w), (zh * 4 + (x + 3) % 4, w)
    partner = ((1 - zh) * 4 + x, w)
    up, down = (t, zl * 8 + ((y + 1) % 4) * 2 + c), (t, zl * 8 + ((y + 3) % 4) * 2 + c)
    sibling = (t, zl * 8 + y * 2 + 1 - c)
    across = (t, (1 - zl) * 8 + y * 2 + c)

    def remote(src, dst, send, recv, target):
        return pltpu.make_async_remote_copy(src_ref=src, dst_ref=dst, send_sem=send, recv_sem=recv, device_id=target, device_id_type=MESH)

    def gather(src, unit, half, target, sem):
        ref = {0: qx, 1: qg}.get(src, qbuf.at[src])
        rows = pl.ds(0, 128) if half is None else pl.ds(half * 64, 64)
        return remote(ref.at[rows], qbuf.at[unit, rows], ag_send.at[sem], ag_recv.at[unit, half or 0], target)

    own = [gather(0, 3, None, right, 0), gather(0, 4, None, left, 1), gather(0, 2, None, partner, 2),
           gather(1, 6, None, right, 3), gather(1, 7, None, left, 4), gather(1, 5, None, partner, 5)]
    forward = {
        2: [gather(2, 8, None, right, 6), gather(2, 9, None, left, 7)],
        3: [gather(3, 10, 0, right, 8)],
        4: [gather(4, 10, 1, left, 9)],
        6: [gather(6, 11, 0, right, 10), gather(6, 12, None, partner, 11)],
        7: [gather(7, 11, 1, left, 12), gather(7, 13, None, partner, 13)],
        8: [gather(8, 14, 0, right, 14)],
        9: [gather(9, 14, 1, left, 15)],
        12: [gather(12, 15, 0, right, 16)],
        13: [gather(13, 15, 1, left, 17)],
    }

    def load(matrix, s, half):
        row = pl.multiple_of(half * 1024 + ((y + REL[s]) % 4) * 256, 256)
        slot = (s * 2 + half) % STAGES
        return pltpu.make_async_copy((rx, rg)[matrix].at[pl.ds(row, 256)], stage.at[slot], stage_sem.at[slot])

    def split(matrix, s):
        for half in range(2):
            slot = (s * 2 + half) % STAGES
            load(matrix, s, half).wait()
            value = stage[slot]
            hi = value.astype(BF16)
            rh[matrix, s, pl.ds(half * 256, 256)] = hi
            rl[matrix, s, pl.ds(half * 256, 256)] = (value - hi.astype(F32)).astype(BF16)
            later = s * 2 + half + STAGES
            if matrix * 8 + later < 16:
                load(matrix + later // 8, (later % 8) // 2, half).start()

    barrier = pltpu.get_barrier_semaphore()
    others = (right, left, partner, up, down, sibling, across)
    for other in others:
        pl.semaphore_signal(barrier, inc=1, device_id=other, device_id_type=MESH)
    mine = [pltpu.make_async_copy(qx, qbuf.at[0], load_sem.at[0]), pltpu.make_async_copy(qg, qbuf.at[1], load_sem.at[1])]
    mine[0].start()
    for s in range(2):
        for half in range(2):
            load(0, s, half).start()
    mine[1].start()
    pl.semaphore_wait(barrier, len(others))
    for copy in own:
        copy.start()

    def core_copy(u, s):
        return remote(pbuf.at[s, 1 - c], csum.at[u, s], c_send.at[s], c_recv.at[u, s], sibling)

    def y1_copies(u):
        return (remote(csum.at[u, 0, 0], y1.at[u, 0], y1_send.at[u, 0], y1_recv.at[u, 0], up),
                remote(csum.at[u, 0, 1], y1.at[u, 1], y1_send.at[u, 1], y1_recv.at[u, 1], down))

    def y2_copies(u):
        return (remote(csum.at[u, 1], y2.at[u, 0], y2_send.at[u, 0], y2_recv.at[u, 0], up),
                remote(csum.at[u, 2], y2.at[u, 1], y2_send.at[u, 1], y2_recv.at[u, 1], down))

    def z_copy(u):
        return remote(csum.at[u, 3, 1 - zl], zin.at[u], z_send.at[u], z_recv.at[u], across)

    def arrive(k):
        if k < 2:
            mine[k].wait()
            return
        for half in (0, 1) if k in HALVED else (None,):
            gather(2, k, half, right, 0).wait_recv()
        for copy in forward.get(k, ()):
            copy.start()

    def core_stage(u, s):
        core_copy(u, s).wait_recv()
        csum[u, s] += pbuf[s, c]
        if s == 0:
            for copy in y1_copies(u):
                copy.start()

    def y1_stage(u):
        for i, (first, second) in enumerate(zip(y1_copies(u), y2_copies(u))):
            first.wait_recv()
            csum[u, 1 + i, i] += y1[u, i]
            second.start()

    def y2_stage(u):
        for copy in y2_copies(u):
            copy.wait_recv()
        csum[u, 3] += y2[u, 0] + y2[u, 1]
        z_copy(u).start()

    def unit(u, carry):
        matrix = ((u + 1) // 3 + 1 + u // 15 + (15 - u) // 15) % 2
        for k in range(UNITS):
            pl.when(u == k)(functools.partial(arrive, k))
        value = qbuf[u]
        hi = value.astype(BF16)
        qcat[pl.ds(0, 128)] = hi
        qcat[pl.ds(128, 128)] = (value - hi.astype(F32)).astype(BF16)
        for s in range(4):
            for k in range(2):
                pl.when(u == k)(functools.partial(split, k, s))

            @pl.when(u >= 1)
            def _():
                core_copy(u - 1, s).wait_send()

            q = qcat[...]
            product = lax.dot_general(rh[matrix, s], q, NT, preferred_element_type=F32)
            product += lax.dot_general(rl[matrix, s], q, NT, preferred_element_type=F32)
            product = product[:, :128] + product[:, 128:]
            for i in range(4):
                pbuf[s, i % 2, i // 2] = product[i * 128:(i + 1) * 128]
            core_copy(u, s).start()
            if s >= 2:
                core_stage(u, s - 2)
            else:
                pl.when(u >= 1)(functools.partial(core_stage, u - 1, s + 2))
            if s == 2:
                pl.when(u >= 1)(functools.partial(y1_stage, u - 1))
            if s == 0:
                pl.when(u >= 3)(functools.partial(y2_stage, u - 3))
        return carry

    lax.fori_loop(0, UNITS, unit, 0)
    last = UNITS - 1
    core_stage(last, 2)
    core_stage(last, 3)
    y1_stage(last)

    def gram(u):
        z_copy(u).wait_recv()
        return csum[u, 3, zl] + zin[u]

    def finish(block):
        first, second, dx, flip = block
        source = ((zh + flip) % 2) * 4 + (x + dx) % 4
        out[:, pl.ds(pl.multiple_of(source * 128, 128), 128)] = gram(first) * gram(second)

    y2_stage(last - 2)
    for block in BLOCKS[:6]:
        finish(block)
    y2_stage(last - 1)
    finish(BLOCKS[6])
    y2_stage(last)
    finish(BLOCKS[7])

    for copy in own + [copy for copies in forward.values() for copy in copies]:
        copy.wait_send()
    for s in range(4):
        core_copy(last, s).wait_send()

    def drain(u, carry):
        for copy in (*y1_copies(u), *y2_copies(u), z_copy(u)):
            copy.wait_send()
        return carry

    lax.fori_loop(0, UNITS, drain, 0)


def per_device(resident_x, resident_g, query_x, query_g):
    dma = pltpu.SemaphoreType.DMA
    return pl.pallas_call(
        kernel,
        out_shape=jax.ShapeDtypeStruct((128, 1024), F32),
        in_specs=[pl.BlockSpec(memory_space=pl.ANY)] * 4,
        out_specs=pl.BlockSpec(memory_space=pltpu.VMEM),
        scratch_shapes=[
            pltpu.VMEM((2, 4, 512, 1024), BF16),
            pltpu.VMEM((2, 4, 512, 1024), BF16),
            pltpu.VMEM((UNITS, 128, 1024), F32),
            pltpu.VMEM((256, 1024), BF16),
            pltpu.VMEM((STAGES, 256, 1024), F32),
            pltpu.VMEM((4, 2, 2, 128, 128), F32),
            pltpu.VMEM((UNITS, 4, 2, 128, 128), F32),
            pltpu.VMEM((UNITS, 2, 128, 128), F32),
            pltpu.VMEM((UNITS, 2, 2, 128, 128), F32),
            pltpu.VMEM((UNITS, 128, 128), F32),
            dma((2,)), dma((STAGES,)), dma((18,)), dma((UNITS, 2)), dma((4,)), dma((UNITS, 4)),
            dma((UNITS, 2)), dma((UNITS, 2)), dma((UNITS, 2)), dma((UNITS, 2)), dma((UNITS,)), dma((UNITS,)),
        ],
        compiler_params=pltpu.CompilerParams(collective_id=0, has_side_effects=True, vmem_limit_bytes=58 * 2**20),
    )(resident_x, resident_g, query_x, query_g)


def solution(mesh):
    return jax.shard_map(
        per_device,
        mesh=mesh,
        in_specs=(P("tok", "wid"), P("tok", "wid"), P("tok", "wid"), P("tok", "wid")),
        out_specs=P(("tok", "wid"), None),
        check_vma=False,
    )
```

```python
import functools

import jax
import jax.numpy as jnp
from jax import lax
from jax.experimental import pallas as pl
from jax.experimental.pallas import tpu as pltpu
from jax.sharding import PartitionSpec as P

MESH = pl.DeviceIdType.MESH
F32, BF16 = jnp.float32, jnp.bfloat16
NT = (((1,), (1,)), ((), ()))

BLOCKS = ((0, 1, 0, 0), (4, 7, 0, 1), (8, 11, 2, 0), (9, 12, 3, 1), (10, 13, 1, 1), (14, 15, 2, 1))
EAGER = 4
UNITS = 16
REL = (2, 1, 3, 0)
STAGES = 8
PARTS = ((0, 1), (1, 3), (3, 4))


def kernel(rx, rg, qx, qg, out, rh, rl, qbuf, qcat, stage, pbuf, csum, y1, y2, zin,
           load_sem, stage_sem, ag_send, ag_recv, c_send, c_recv, y1_send, y1_recv, y2_send, y2_recv, z_send, z_recv):
    t, w = lax.axis_index("tok"), lax.axis_index("wid")
    zh, x = t // 4, t % 4
    zl, y, c = w // 8, (w // 2) % 4, w % 2
    right, left = (zh * 4 + (x + 1) % 4, w), (zh * 4 + (x + 3) % 4, w)
    partner = ((1 - zh) * 4 + x, w)
    up, down = (t, zl * 8 + ((y + 1) % 4) * 2 + c), (t, zl * 8 + ((y + 3) % 4) * 2 + c)
    sibling = (t, zl * 8 + y * 2 + 1 - c)
    across = (t, (1 - zl) * 8 + y * 2 + c)

    def remote(src, dst, send, recv, target):
        return pltpu.make_async_remote_copy(src_ref=src, dst_ref=dst, send_sem=send, recv_sem=recv, device_id=target, device_id_type=MESH)

    def gather(src, start, unit, row, rows, target):
        ref = {0: qx, 1: qg}.get(src, qbuf.at[src])
        return remote(ref.at[pl.ds(start, rows)], qbuf.at[unit, pl.ds(row, rows)], ag_send, ag_recv.at[unit], target)

    own = []
    for m in range(2):
        own += [gather(m, 0, 2 + 3 * m, 0, 64, right), gather(m, 0, 2 + 3 * m, 64, 64, left), gather(m, 0, 4 + 3 * m, 0, 128, partner),
                gather(m, 64, 3 + 3 * m, 0, 64, right), gather(m, 64, 3 + 3 * m, 64, 64, left)]
    forward = {
        2: [gather(2, 0, 8, 0, 64, right)],
        3: [gather(3, 64, 8, 64, 64, left)],
        4: [gather(4, 0, 9, 0, 128, right), gather(4, 0, 10, 0, 128, left)],
        5: [gather(5, 0, 12, 0, 64, partner), gather(5, 64, 13, 0, 64, partner), gather(5, 0, 11, 0, 64, right)],
        6: [gather(6, 0, 12, 64, 64, partner), gather(6, 64, 13, 64, 64, partner), gather(6, 64, 11, 64, 64, left)],
        9: [gather(9, 0, 14, 0, 64, right)],
        10: [gather(10, 64, 14, 64, 64, left)],
        12: [gather(12, 0, 15, 0, 64, right)],
        13: [gather(13, 64, 15, 64, 64, left)],
    }

    def load(matrix, s, half):
        row = pl.multiple_of(half * 1024 + ((y + REL[s]) % 4) * 256, 256)
        slot = (s * 2 + half) % STAGES
        return pltpu.make_async_copy((rx, rg)[matrix].at[pl.ds(row, 256)], stage.at[slot], stage_sem.at[slot])

    def split(matrix, s):
        for half in range(2):
            slot = (s * 2 + half) % STAGES
            load(matrix, s, half).wait()
            value = stage[slot]
            hi = value.astype(BF16)
            rh[matrix, s, pl.ds(half * 256, 256)] = hi
            rl[matrix, s, pl.ds(half * 256, 256)] = (value - hi.astype(F32)).astype(BF16)
            if matrix == 0:
                load(1, s, half).start()

    barrier = pltpu.get_barrier_semaphore()
    others = (right, left, partner, up, down, sibling, across)
    for other in others:
        pl.semaphore_signal(barrier, inc=1, device_id=other, device_id_type=MESH)
    mine = [pltpu.make_async_copy(qx, qbuf.at[0], load_sem.at[0]), pltpu.make_async_copy(qg, qbuf.at[1], load_sem.at[1])]
    mine[0].start()
    for s in range(4):
        for half in range(2):
            load(0, s, half).start()
    mine[1].start()

    def core_copy(u, lo, hi):
        parts, part = pl.ds(lo, hi - lo), (lo + 1) // 2
        return remote(pbuf.at[u % 2, 1 - c, parts], csum.at[u, parts], c_send.at[u % 2, part], c_recv.at[UNITS + 2 * u + part - 1 if part else u], sibling)

    def y1_copies(u):
        return (remote(csum.at[u, 0, 0], y1.at[u, 0], y1_send, y1_recv.at[u], up),
                remote(csum.at[u, 0, 1], y1.at[u, 1], y1_send, y1_recv.at[u], down))

    def y2_copies(u):
        return (remote(csum.at[u, 1], y2.at[u, 0], y2_send, y2_recv.at[u], up),
                remote(csum.at[u, 2], y2.at[u, 1], y2_send, y2_recv.at[u], down))

    def z_copy(u):
        return remote(csum.at[u, 3, 1 - zl], zin.at[u], z_send, z_recv.at[u], across)

    def arrive(k):
        remote(qbuf.at[k], qbuf.at[k], ag_send, ag_recv.at[k], right).wait_recv()
        for copy in forward.get(k, ()):
            copy.start()

    def core_stage(u, lo, hi):
        core_copy(u, lo, hi).wait_recv()
        for s in range(lo, hi):
            csum[u, s] += pbuf[u % 2, c, s]
            if s == 0:
                for copy in y1_copies(u):
                    copy.start()

    def y1_stage(u):
        remote(y1.at[u], y1.at[u], y1_send, y1_recv.at[u], up).wait_recv()
        for i, copy in enumerate(y2_copies(u)):
            csum[u, 1 + i, i] += y1[u, i]
            copy.start()

    def y2_stage(u):
        remote(y2.at[u], y2.at[u], y2_send, y2_recv.at[u], up).wait_recv()
        csum[u, 3] += y2[u, 0] + y2[u, 1]
        z_copy(u).start()

    def queries(u, slot):
        value = qbuf[u]
        hi = value.astype(BF16)
        qcat[slot, pl.ds(0, 128)] = hi
        qcat[slot, pl.ds(128, 128)] = (value - hi.astype(F32)).astype(BF16)

    def dots(u, matrix, lo, hi):
        q = qcat[u if isinstance(u, int) else 0]
        for s in range(lo, hi):
            product = lax.dot_general(rh[matrix, s], q, NT, preferred_element_type=F32)
            product += lax.dot_general(rl[matrix, s], q, NT, preferred_element_type=F32)
            product = product[:, :128] + product[:, 128:]
            for i in range(4):
                pbuf[u % 2, i % 2, s, i // 2] = product[i * 128:(i + 1) * 128]

    def send(u, lo, hi):
        core_copy(u, lo, hi).start()

    mine[0].wait()
    queries(0, 0)
    split(0, 0)
    dots(0, 0, 0, 1)
    pl.semaphore_wait(barrier, len(others))
    send(0, 0, 1)
    for copy in own:
        copy.start()
    split(0, 1)
    split(0, 2)
    core_stage(0, 0, 1)
    dots(0, 0, 1, 3)
    send(0, 1, 3)
    mine[1].wait()
    queries(1, 1)
    split(1, 0)
    split(0, 3)
    core_stage(0, 1, 3)
    y1_stage(0)
    dots(1, 1, 0, 1)
    send(1, 0, 1)
    dots(0, 0, 3, 4)
    send(0, 3, 4)
    core_stage(1, 0, 1)
    split(1, 1)
    split(1, 2)
    dots(1, 1, 1, 3)
    send(1, 1, 3)
    split(1, 3)
    core_stage(0, 3, 4)
    core_stage(1, 1, 3)
    y1_stage(1)
    dots(1, 1, 3, 4)
    send(1, 3, 4)
    for lo, hi in PARTS:
        core_copy(0, lo, hi).wait_send()

    def stages(u):
        @pl.when(u >= 3)
        def _():
            core_stage(u - 1, 0, 4)
            core_copy(u - 1, 0, 4).wait_send()

        @pl.when(u >= 4)
        def _():
            y1_stage(u - 2)

    def unit(u, carry):
        matrix = ((u + 1) // 3 + 1 + u // 15) % 2
        pl.when(u <= EAGER)(functools.partial(stages, u))
        for k in range(2, UNITS):
            pl.when(u == k)(functools.partial(arrive, k))
        queries(u, 0)
        dots(u, matrix, 0, 4)
        send(u, 0, 4)

        @pl.when(u == 2)
        def _():
            core_stage(1, 3, 4)
            for lo, hi in PARTS:
                core_copy(1, lo, hi).wait_send()

        pl.when(u > EAGER)(functools.partial(stages, u))

        @pl.when((u >= 9) & (u < 14))
        def _():
            y2_stage(2 * (u - 9))
            y2_stage(2 * (u - 9) + 1)

        @pl.when(u >= 14)
        def _():
            y2_stage(u - 4)

        return carry

    lax.fori_loop(2, UNITS, unit, 0)
    last = UNITS - 1
    core_stage(last, 0, 4)
    y1_stage(last - 1)
    y2_stage(last - 3)
    y1_stage(last)

    def gram(u):
        z_copy(u).wait_recv()
        return csum[u, 3, zl] + zin[u]

    def store(dx, flip, value):
        source = ((zh + flip) % 2) * 4 + (x + dx) % 4
        out[:, pl.ds(pl.multiple_of(source * 128, 128), 128)] = value

    def finish(block):
        first, second, dx, flip = block
        store(dx, flip, gram(first) * gram(second))

    y2_stage(last - 2)
    halves = gram(2) * gram(5), gram(3) * gram(6)
    store(3, 0, jnp.concatenate([half[:, :64] for half in halves], axis=1))
    store(1, 0, jnp.concatenate([half[:, 64:] for half in halves], axis=1))
    for block in BLOCKS[:4]:
        finish(block)
    y2_stage(last - 1)
    finish(BLOCKS[4])
    y2_stage(last)
    finish(BLOCKS[5])

    core_copy(last, 0, 4).wait_send()
    everything = qbuf.at[pl.ds(2, UNITS - 2)]
    for ref, sem in ((everything, ag_send), (y1, y1_send), (y2, y2_send), (zin, z_send)):
        remote(ref, ref, sem, sem, right).wait_send()


def per_device(resident_x, resident_g, query_x, query_g):
    dma = pltpu.SemaphoreType.DMA
    return pl.pallas_call(
        kernel,
        out_shape=jax.ShapeDtypeStruct((128, 1024), F32),
        in_specs=[pl.BlockSpec(memory_space=pl.ANY)] * 4,
        out_specs=pl.BlockSpec(memory_space=pltpu.VMEM),
        scratch_shapes=[
            pltpu.VMEM((2, 4, 512, 1024), BF16),
            pltpu.VMEM((2, 4, 512, 1024), BF16),
            pltpu.VMEM((UNITS, 128, 1024), F32),
            pltpu.VMEM((2, 256, 1024), BF16),
            pltpu.VMEM((STAGES, 256, 1024), F32),
            pltpu.VMEM((2, 2, 4, 2, 128, 128), F32),
            pltpu.VMEM((UNITS, 4, 2, 128, 128), F32),
            pltpu.VMEM((UNITS, 2, 128, 128), F32),
            pltpu.VMEM((UNITS, 2, 2, 128, 128), F32),
            pltpu.VMEM((UNITS, 128, 128), F32),
            dma((2,)), dma((STAGES,)), dma, dma((UNITS,)), dma((2, 3)), dma((UNITS + 4,)),
            dma, dma((UNITS,)), dma, dma((UNITS,)), dma, dma((UNITS,)),
        ],
        compiler_params=pltpu.CompilerParams(collective_id=0, has_side_effects=True, vmem_limit_bytes=58 * 2**20),
    )(resident_x, resident_g, query_x, query_g)


def solution(mesh):
    return jax.shard_map(
        per_device,
        mesh=mesh,
        in_specs=(P("tok", "wid"), P("tok", "wid"), P("tok", "wid"), P("tok", "wid")),
        out_specs=P(("tok", "wid"), None),
        check_vma=False,
    )
```

```python
import functools

import jax
import jax.numpy as jnp
from jax import lax
from jax.experimental import pallas as pl
from jax.experimental.pallas import tpu as pltpu
from jax.sharding import PartitionSpec as P

MESH = pl.DeviceIdType.MESH
F32, BF16 = jnp.float32, jnp.bfloat16
NT = (((1,), (1,)), ((), ()))

BLOCKS = ((0, 1, 0, 0), (4, 7, 0, 1), (8, 11, 2, 0), (9, 12, 3, 1), (10, 13, 1, 1), (14, 15, 2, 1))
ACROSS_FIRST = (11, 13)
STEPS = ("CyAY", "ACyZW", "yACy", "ACZW", "yACyZ", "ACyW", "ACYCZZZ", "YCAYW", "YAYW", "CyAyC", "AyC", "ACY", "ACYZ", "yAyC")
LAST = "ZCWYWZZYZYZYZZZZZ"
UNITS = 16
REL = (2, 1, 3, 0)
STAGES = 16
PARTS = ((0, 1), (1, 3), (3, 4))


def kernel(rx, rg, qx, qg, out, rh, rl, qbuf, qcat, stage, pbuf, csum, y1, y2, zin, zfirst,
           load_sem, stage_sem, ag_send, ag_recv, c_send, c_recv, y1_send, y1_recv, y2_send, y2_recv, z_send, z_recv, first_send, first_recv):
    t, w = lax.axis_index("tok"), lax.axis_index("wid")
    zh, x = t // 4, t % 4
    zl, y, c = w // 8, (w // 2) % 4, w % 2
    right, left = (zh * 4 + (x + 1) % 4, w), (zh * 4 + (x + 3) % 4, w)
    partner = ((1 - zh) * 4 + x, w)
    up, down = (t, zl * 8 + ((y + 1) % 4) * 2 + c), (t, zl * 8 + ((y + 3) % 4) * 2 + c)
    sibling = (t, zl * 8 + y * 2 + 1 - c)
    across = (t, (1 - zl) * 8 + y * 2 + c)

    def remote(src, dst, send, recv, target):
        return pltpu.make_async_remote_copy(src_ref=src, dst_ref=dst, send_sem=send, recv_sem=recv, device_id=target, device_id_type=MESH)

    def gather(src, start, unit, row, rows, target):
        ref = {0: qx, 1: qg}.get(src, qbuf.at[src])
        return remote(ref.at[pl.ds(start, rows)], qbuf.at[unit, pl.ds(row, rows)], ag_send, ag_recv.at[unit], target)

    own = []
    for m in range(2):
        own += [gather(m, 0, 2 + 3 * m, 0, 64, right), gather(m, 0, 2 + 3 * m, 64, 64, left), gather(m, 0, 4 + 3 * m, 0, 128, partner),
                gather(m, 64, 3 + 3 * m, 0, 64, right), gather(m, 64, 3 + 3 * m, 64, 64, left)]
    forward = {
        2: [gather(2, 0, 8, 0, 64, right)],
        3: [gather(3, 64, 8, 64, 64, left)],
        4: [gather(4, 0, 9, 0, 128, right), gather(4, 0, 10, 0, 128, left)],
        5: [gather(5, 0, 12, 0, 64, partner), gather(5, 64, 13, 0, 64, partner), gather(5, 0, 11, 0, 64, right)],
        6: [gather(6, 0, 12, 64, 64, partner), gather(6, 64, 13, 64, 64, partner), gather(6, 64, 11, 64, 64, left)],
        9: [gather(9, 0, 14, 0, 64, right)],
        10: [gather(10, 64, 14, 64, 64, left)],
        12: [gather(12, 0, 15, 0, 64, right)],
        13: [gather(13, 64, 15, 64, 64, left)],
    }

    def load(matrix, s, half):
        row = pl.multiple_of(half * 1024 + ((y + REL[s]) % 4) * 256, 256)
        slot = matrix * 8 + s * 2 + half
        return pltpu.make_async_copy((rx, rg)[matrix].at[pl.ds(row, 256)], stage.at[slot], stage_sem.at[slot])

    def split(matrix, *parts):
        for s in parts:
            for half in range(2):
                load(matrix, s, half).wait()
        for s in parts:
            for half in range(2):
                value = stage[matrix * 8 + s * 2 + half]
                hi = value.astype(BF16)
                rh[matrix, s, pl.ds(half * 256, 256)] = hi
                rl[matrix, s, pl.ds(half * 256, 256)] = (value - hi.astype(F32)).astype(BF16)

    barrier = pltpu.get_barrier_semaphore()
    others = (right, left, partner, up, down, sibling, across)
    for other in others:
        pl.semaphore_signal(barrier, inc=1, device_id=other, device_id_type=MESH)
    mine = [pltpu.make_async_copy(qx, qbuf.at[0], load_sem.at[0]), pltpu.make_async_copy(qg, qbuf.at[1], load_sem.at[1])]
    mine[0].start()
    for matrix, s in ((0, 0), (0, 1), (0, 2), (1, 0), (0, 3), (1, 1), (1, 2), (1, 3)):
        for half in range(2):
            load(matrix, s, half).start()
    mine[1].start()

    def core_copy(u, lo, hi):
        parts, part = pl.ds(lo, hi - lo), (lo + 1) // 2
        return remote(pbuf.at[u % 2, 1 - c, parts], csum.at[u, parts], c_send.at[u % 2, part], c_recv.at[UNITS + 2 * u + part - 1 if part else u], sibling)

    def y1_copies(u):
        if u in ACROSS_FIRST:
            low, high = pl.ds(0, 64), pl.ds(64, 64)
            return (remote(csum.at[u, 0, zl, low], y1.at[u, 0, low], y1_send, y1_recv.at[u], up),
                    remote(csum.at[u, 0, zl, high], y1.at[u, 1, high], y1_send, y1_recv.at[u], down))
        return (remote(csum.at[u, 0, 0], y1.at[u, 0], y1_send, y1_recv.at[u], up),
                remote(csum.at[u, 0, 1], y1.at[u, 1], y1_send, y1_recv.at[u], down))

    def y2_copies(u):
        if u in ACROSS_FIRST:
            return (remote(csum.at[u, 1, zl], y2.at[u, 0, 0], y2_send, y2_recv.at[u], up),
                    remote(csum.at[u, 2, zl], y2.at[u, 1, 0], y2_send, y2_recv.at[u], down))
        return (remote(csum.at[u, 1], y2.at[u, 0], y2_send, y2_recv.at[u], up),
                remote(csum.at[u, 2], y2.at[u, 1], y2_send, y2_recv.at[u], down))

    def z_copy(u):
        return remote(csum.at[u, 3, 1 - zl], zin.at[u], z_send, z_recv.at[u], across)

    def first_copy(u):
        i = ACROSS_FIRST.index(u)
        return remote(csum.at[u, :, 1 - zl], zfirst.at[i], first_send, first_recv.at[i], across)

    def arrive(k):
        remote(qbuf.at[k], qbuf.at[k], ag_send, ag_recv.at[k], right).wait_recv()
        for copy in forward.get(k, ()):
            copy.start()

    def core_stage(u, lo, hi):
        core_copy(u, lo, hi).wait_recv()
        for s in range(lo, hi):
            csum[u, s] += pbuf[u % 2, c, s]
            if s == 0 and u not in ACROSS_FIRST:
                for copy in y1_copies(u):
                    copy.start()
        if u in ACROSS_FIRST:
            first_copy(u).start()

    def across_stage(u):
        first_copy(u).wait_recv()
        for s in range(4):
            csum[u, s, zl] += zfirst[ACROSS_FIRST.index(u), s]
            if s == 0:
                for copy in y1_copies(u):
                    copy.start()

    def y1_stage(u):
        half = u in ACROSS_FIRST
        landed = y1.at[u, :, pl.ds(0, 64)] if half else y1.at[u]
        remote(landed, landed, y1_send, y1_recv.at[u], up).wait_recv()
        for i, copy in enumerate(y2_copies(u)):
            if half:
                rows = pl.ds(i * 64, 64)
                csum[u, 1 + i, zl, rows] += y1[u, i, rows]
            else:
                csum[u, 1 + i, i] += y1[u, i]
            copy.start()

    def y2_stage(u):
        half = u in ACROSS_FIRST
        landed = y2.at[u, :, 0] if half else y2.at[u]
        remote(landed, landed, y2_send, y2_recv.at[u], up).wait_recv()
        if half:
            csum[u, 3, zl] += y2[u, 0, 0] + y2[u, 1, 0]
        else:
            csum[u, 3] += y2[u, 0] + y2[u, 1]
            z_copy(u).start()

    def queries(u, slot):
        value = qbuf[u]
        hi = value.astype(BF16)
        qcat[slot, pl.ds(0, 128)] = hi
        qcat[slot, pl.ds(128, 128)] = (value - hi.astype(F32)).astype(BF16)

    def dots(u, matrix, lo, hi):
        q = qcat[u if isinstance(u, int) else 0]
        for s in range(lo, hi):
            product = lax.dot_general(rh[matrix, s], q, NT, preferred_element_type=F32)
            product += lax.dot_general(rl[matrix, s], q, NT, preferred_element_type=F32)
            product = product[:, :128] + product[:, 128:]
            for i in range(4):
                pbuf[u % 2, i % 2, s, i // 2] = product[i * 128:(i + 1) * 128]

    def send(u, lo, hi):
        core_copy(u, lo, hi).start()

    mine[0].wait()
    queries(0, 0)
    split(0, 0)
    dots(0, 0, 0, 1)
    pl.semaphore_wait(barrier, len(others))
    send(0, 0, 1)
    for copy in own:
        copy.start()
    mine[1].wait()
    queries(1, 1)
    split(0, 1, 2)
    split(1, 0)
    core_stage(0, 0, 1)
    dots(1, 1, 0, 1)
    send(1, 0, 1)
    dots(0, 0, 1, 3)
    send(0, 1, 3)
    core_stage(1, 0, 1)
    split(1, 1, 2)
    core_stage(0, 1, 3)
    y1_stage(0)
    dots(1, 1, 1, 3)
    send(1, 1, 3)
    split(0, 3)
    split(1, 3)
    dots(0, 0, 3, 4)
    send(0, 3, 4)
    core_stage(1, 1, 3)
    y1_stage(1)

    summed, on_y1, on_y2, on_z = 1, [], [0, 1], []
    done = []

    def plan(steps):
        nonlocal summed
        todo = []
        for step in steps:
            if step == "C" and summed < ready:
                summed += 1
                todo.append((core_stage, summed, 0, 4))
                (on_z if summed in ACROSS_FIRST else on_y1).append(summed)
            elif step == "W" and on_z:
                todo.append((across_stage, on_z[0]))
                on_y1.append(on_z.pop(0))
            elif step in "Yy" and len(on_y1) > (step == "y"):
                todo.append((y1_stage, on_y1[0]))
                on_y2.append(on_y1.pop(0))
            elif step == "Z" and on_y2:
                todo.append((y2_stage, on_y2[0]))
                done.append(on_y2.pop(0))
        return todo

    before, after = {}, {}
    for k in range(2, UNITS):
        ready = k - 1
        first, second = STEPS[k - 2].split("A")
        before[k] = plan(first)
        assert summed >= k - 2
        ready = k
        after[k] = plan(second)
    ending = plan(LAST + "CC" + "WYWY" + "Y" * UNITS + "Z" * UNITS)

    def carry_out(todo):
        for stage_of, *which in todo:
            stage_of(*which)

    def begin(k):
        if k < 4:
            core_stage(k - 2, 3, 4)
        carry_out(before[k])
        arrive(k)
        for lo, hi in PARTS if k < 4 else ((0, 4),):
            core_copy(k - 2, lo, hi).wait_send()

    def end(k):
        if k == 2:
            dots(1, 1, 3, 4)
            send(1, 3, 4)
        carry_out(after[k])

    def unit(u, carry):
        matrix = ((u + 1) // 3 + 1 + u // 15) % 2
        for k in range(2, UNITS):
            pl.when(u == k)(functools.partial(begin, k))
        queries(u, 0)
        dots(u, matrix, 0, 4)
        send(u, 0, 4)
        for k in range(2, UNITS):
            pl.when(u == k)(functools.partial(end, k))
        return carry

    lax.fori_loop(2, UNITS, unit, 0)
    last = UNITS - 1
    carry_out(ending)

    def gram(u):
        if u in ACROSS_FIRST:
            return csum[u, 3, zl]
        z_copy(u).wait_recv()
        return csum[u, 3, zl] + zin[u]

    def store(dx, flip, value):
        source = ((zh + flip) % 2) * 4 + (x + dx) % 4
        out[:, pl.ds(pl.multiple_of(source * 128, 128), 128)] = value

    def finish(block):
        first, second, dx, flip = block
        store(dx, flip, gram(first) * gram(second))

    halves = gram(2) * gram(5), gram(3) * gram(6)
    store(3, 0, jnp.concatenate([half[:, :64] for half in halves], axis=1))
    store(1, 0, jnp.concatenate([half[:, 64:] for half in halves], axis=1))
    for block in sorted(BLOCKS, key=lambda block: max(done.index(u) for u in block[:2])):
        finish(block)

    for u in (last - 1, last):
        core_copy(u, 0, 4).wait_send()
    whole = pl.ds(0, UNITS - len(ACROSS_FIRST) // 2)
    for ref, sem in ((qbuf.at[pl.ds(2, UNITS - 2)], ag_send), (y1.at[whole], y1_send), (y2.at[whole], y2_send),
                     (zin.at[pl.ds(0, UNITS - len(ACROSS_FIRST))], z_send), (zfirst, first_send)):
        remote(ref, ref, sem, sem, right).wait_send()


def per_device(resident_x, resident_g, query_x, query_g):
    dma = pltpu.SemaphoreType.DMA
    return pl.pallas_call(
        kernel,
        out_shape=jax.ShapeDtypeStruct((128, 1024), F32),
        in_specs=[pl.BlockSpec(memory_space=pl.ANY)] * 4,
        out_specs=pl.BlockSpec(memory_space=pltpu.VMEM),
        scratch_shapes=[
            pltpu.VMEM((2, 4, 512, 1024), BF16),
            pltpu.VMEM((2, 4, 512, 1024), BF16),
            pltpu.VMEM((UNITS, 128, 1024), F32),
            pltpu.VMEM((2, 256, 1024), BF16),
            pltpu.VMEM((STAGES, 256, 1024), F32),
            pltpu.VMEM((2, 2, 4, 2, 128, 128), F32),
            pltpu.VMEM((UNITS, 4, 2, 128, 128), F32),
            pltpu.VMEM((UNITS, 2, 128, 128), F32),
            pltpu.VMEM((UNITS, 2, 2, 128, 128), F32),
            pltpu.VMEM((UNITS, 128, 128), F32),
            pltpu.VMEM((len(ACROSS_FIRST), 4, 128, 128), F32),
            dma((2,)), dma((STAGES,)), dma, dma((UNITS,)), dma((2, 3)), dma((UNITS + 4,)),
            dma, dma((UNITS,)), dma, dma((UNITS,)), dma, dma((UNITS,)), dma, dma((len(ACROSS_FIRST),)),
        ],
        compiler_params=pltpu.CompilerParams(collective_id=0, has_side_effects=True, vmem_limit_bytes=61 * 2**20),
    )(resident_x, resident_g, query_x, query_g)


def solution(mesh):
    return jax.shard_map(
        per_device,
        mesh=mesh,
        in_specs=(P("tok", "wid"), P("tok", "wid"), P("tok", "wid"), P("tok", "wid")),
        out_specs=P(("tok", "wid"), None),
        check_vma=False,
    )
```

```python
import functools

import jax
import jax.numpy as jnp
from jax import lax
from jax.experimental import pallas as pl
from jax.experimental.pallas import tpu as pltpu
from jax.sharding import PartitionSpec as P

MESH = pl.DeviceIdType.MESH
F32, BF16 = jnp.float32, jnp.bfloat16
NT = (((1,), (1,)), ((), ()))

BLOCKS = ((0, 1, 0, 0), (4, 7, 0, 1), (8, 11, 2, 0), (9, 12, 3, 1), (10, 13, 1, 1), (14, 15, 2, 1))
ACROSS_FIRST = (11, 13)
STEPS = ("CyAY", "ACyZW", "yACy", "ACZW", "yACyZ", "ACyW", "ACYCZZZ", "YCAYW", "YAYW", "CyAyC", "AyC", "ACY", "ACYZ", "yAyC")
LAST = "ZCWYWZZYZYZYZZZZZ"
UNITS = 16
REL = (2, 1, 3, 0)
STAGES = 16
PARTS = ((0, 1), (1, 3), (3, 4))


def kernel(rx, rg, qx, qg, out, rh, rl, qbuf, qcat, stage, pbuf, csum, y1, y2, zin, zfirst,
           load_sem, stage_sem, ag_send, ag_recv, c_send, c_recv, y1_send, y1_recv, y2_send, y2_recv, z_send, z_recv, first_send, first_recv):
    t, w = lax.axis_index("tok"), lax.axis_index("wid")
    zh, x = t // 4, t % 4
    zl, y, c = w // 8, (w // 2) % 4, w % 2
    right, left = (zh * 4 + (x + 1) % 4, w), (zh * 4 + (x + 3) % 4, w)
    partner = ((1 - zh) * 4 + x, w)
    up, down = (t, zl * 8 + ((y + 1) % 4) * 2 + c), (t, zl * 8 + ((y + 3) % 4) * 2 + c)
    sibling = (t, zl * 8 + y * 2 + 1 - c)
    across = (t, (1 - zl) * 8 + y * 2 + c)

    def remote(src, dst, send, recv, target):
        return pltpu.make_async_remote_copy(src_ref=src, dst_ref=dst, send_sem=send, recv_sem=recv, device_id=target, device_id_type=MESH)

    def gather(src, start, unit, row, rows, target):
        ref = {0: qx, 1: qg}.get(src, qbuf.at[src])
        return remote(ref.at[pl.ds(start, rows)], qbuf.at[unit, pl.ds(row, rows)], ag_send, ag_recv.at[unit], target)

    own = []
    for m in range(2):
        own += [gather(m, 0, 2 + 3 * m, 0, 64, right), gather(m, 0, 2 + 3 * m, 64, 64, left), gather(m, 0, 4 + 3 * m, 0, 128, partner),
                gather(m, 64, 3 + 3 * m, 0, 64, right), gather(m, 64, 3 + 3 * m, 64, 64, left)]
    forward = {
        2: [gather(2, 0, 8, 0, 64, right)],
        3: [gather(3, 64, 8, 64, 64, left)],
        4: [gather(4, 0, 9, 0, 128, right), gather(4, 0, 10, 0, 128, left)],
        5: [gather(5, 0, 12, 0, 64, partner), gather(5, 64, 13, 0, 64, partner), gather(5, 0, 11, 0, 64, right)],
        6: [gather(6, 0, 12, 64, 64, partner), gather(6, 64, 13, 64, 64, partner), gather(6, 64, 11, 64, 64, left)],
        9: [gather(9, 0, 14, 0, 64, right)],
        10: [gather(10, 64, 14, 64, 64, left)],
        12: [gather(12, 0, 15, 0, 64, right)],
        13: [gather(13, 64, 15, 64, 64, left)],
    }

    def load(matrix, s, half):
        row = pl.multiple_of(half * 1024 + ((y + REL[s]) % 4) * 256, 256)
        slot = matrix * 8 + s * 2 + half
        return pltpu.make_async_copy((rx, rg)[matrix].at[pl.ds(row, 256)], stage.at[slot], stage_sem.at[slot])

    def split(matrix, *parts):
        for s in parts:
            for half in range(2):
                load(matrix, s, half).wait()
        for s in parts:
            for half in range(2):
                value = stage[matrix * 8 + s * 2 + half]
                hi = value.astype(BF16)
                rh[matrix, s, pl.ds(half * 256, 256)] = hi
                rl[matrix, s, pl.ds(half * 256, 256)] = (value - hi.astype(F32)).astype(BF16)

    barrier = pltpu.get_barrier_semaphore()
    others = (right, left, partner, up, down, sibling, across)
    for other in others:
        pl.semaphore_signal(barrier, inc=1, device_id=other, device_id_type=MESH)
    mine = [pltpu.make_async_copy(qx, qbuf.at[0], load_sem.at[0]), pltpu.make_async_copy(qg, qbuf.at[1], load_sem.at[1])]
    mine[0].start()
    for matrix, s in ((0, 0), (0, 1), (0, 2), (1, 0), (0, 3), (1, 1), (1, 2), (1, 3)):
        for half in range(2):
            load(matrix, s, half).start()
        if (matrix, s) == (0, 0):
            mine[1].start()

    def core_copy(u, lo, hi):
        parts, part = pl.ds(lo, hi - lo), (lo + 1) // 2
        return remote(pbuf.at[u % 2, 1 - c, parts], csum.at[u, parts], c_send.at[u % 2, part], c_recv.at[UNITS + 2 * u + part - 1 if part else u], sibling)

    def y1_copies(u):
        if u in ACROSS_FIRST:
            low, high = pl.ds(0, 64), pl.ds(64, 64)
            return (remote(csum.at[u, 0, zl, low], y1.at[u, 0, low], y1_send, y1_recv.at[u], up),
                    remote(csum.at[u, 0, zl, high], y1.at[u, 1, high], y1_send, y1_recv.at[u], down))
        return (remote(csum.at[u, 0, 0], y1.at[u, 0], y1_send, y1_recv.at[u], up),
                remote(csum.at[u, 0, 1], y1.at[u, 1], y1_send, y1_recv.at[u], down))

    def y2_copies(u):
        if u in ACROSS_FIRST:
            return (remote(csum.at[u, 1, zl], y2.at[u, 0, 0], y2_send, y2_recv.at[u], up),
                    remote(csum.at[u, 2, zl], y2.at[u, 1, 0], y2_send, y2_recv.at[u], down))
        return (remote(csum.at[u, 1], y2.at[u, 0], y2_send, y2_recv.at[u], up),
                remote(csum.at[u, 2], y2.at[u, 1], y2_send, y2_recv.at[u], down))

    def z_copy(u):
        return remote(csum.at[u, 3, 1 - zl], zin.at[u], z_send, z_recv.at[u], across)

    def first_copy(u):
        i = ACROSS_FIRST.index(u)
        return remote(csum.at[u, :, 1 - zl], zfirst.at[i], first_send, first_recv.at[i], across)

    def arrive(k):
        remote(qbuf.at[k], qbuf.at[k], ag_send, ag_recv.at[k], right).wait_recv()
        for copy in forward.get(k, ()):
            copy.start()

    def core_stage(u, lo, hi):
        core_copy(u, lo, hi).wait_recv()
        for s in range(lo, hi):
            csum[u, s] += pbuf[u % 2, c, s]
            if s == 0 and u not in ACROSS_FIRST:
                for copy in y1_copies(u):
                    copy.start()
        if u in ACROSS_FIRST:
            first_copy(u).start()

    def across_stage(u):
        first_copy(u).wait_recv()
        for s in range(4):
            csum[u, s, zl] += zfirst[ACROSS_FIRST.index(u), s]
            if s == 0:
                for copy in y1_copies(u):
                    copy.start()

    def y1_stage(u):
        half = u in ACROSS_FIRST
        landed = y1.at[u, :, pl.ds(0, 64)] if half else y1.at[u]
        remote(landed, landed, y1_send, y1_recv.at[u], up).wait_recv()
        for i, copy in enumerate(y2_copies(u)):
            if half:
                rows = pl.ds(i * 64, 64)
                csum[u, 1 + i, zl, rows] += y1[u, i, rows]
            else:
                csum[u, 1 + i, i] += y1[u, i]
            copy.start()

    def y2_stage(u):
        half = u in ACROSS_FIRST
        landed = y2.at[u, :, 0] if half else y2.at[u]
        remote(landed, landed, y2_send, y2_recv.at[u], up).wait_recv()
        if half:
            csum[u, 3, zl] += y2[u, 0, 0] + y2[u, 1, 0]
        else:
            csum[u, 3] += y2[u, 0] + y2[u, 1]
            z_copy(u).start()

    def queries(u, slot):
        value = qbuf[u]
        hi = value.astype(BF16)
        qcat[slot, pl.ds(0, 128)] = hi
        qcat[slot, pl.ds(128, 128)] = (value - hi.astype(F32)).astype(BF16)

    def dots(u, matrix, lo, hi):
        q = qcat[u if isinstance(u, int) else 0]
        for s in range(lo, hi):
            product = lax.dot_general(rh[matrix, s], q, NT, preferred_element_type=F32)
            product += lax.dot_general(rl[matrix, s], q, NT, preferred_element_type=F32)
            product = product[:, :128] + product[:, 128:]
            for i in range(4):
                pbuf[u % 2, i % 2, s, i // 2] = product[i * 128:(i + 1) * 128]

    def send(u, lo, hi):
        core_copy(u, lo, hi).start()

    mine[0].wait()
    queries(0, 0)
    split(0, 0)
    dots(0, 0, 0, 1)
    pl.semaphore_wait(barrier, len(others))
    send(0, 0, 1)
    for copy in own:
        copy.start()
    mine[1].wait()
    queries(1, 1)
    split(0, 1, 2)
    split(1, 0)
    core_stage(0, 0, 1)
    dots(1, 1, 0, 1)
    send(1, 0, 1)
    dots(0, 0, 1, 3)
    send(0, 1, 3)
    core_stage(1, 0, 1)
    split(1, 1, 2)
    core_stage(0, 1, 3)
    y1_stage(0)
    dots(1, 1, 1, 3)
    send(1, 1, 3)
    split(0, 3)
    split(1, 3)
    dots(0, 0, 3, 4)
    send(0, 3, 4)
    core_stage(1, 1, 3)
    y1_stage(1)

    summed, on_y1, on_y2, on_z = 1, [], [0, 1], []
    done = []

    def plan(steps):
        nonlocal summed
        todo = []
        for step in steps:
            if step == "C" and summed < ready:
                summed += 1
                todo.append((core_stage, summed, 0, 4))
                (on_z if summed in ACROSS_FIRST else on_y1).append(summed)
            elif step == "W" and on_z:
                todo.append((across_stage, on_z[0]))
                on_y1.append(on_z.pop(0))
            elif step in "Yy" and len(on_y1) > (step == "y"):
                todo.append((y1_stage, on_y1[0]))
                on_y2.append(on_y1.pop(0))
            elif step == "Z" and on_y2:
                todo.append((y2_stage, on_y2[0]))
                done.append(on_y2.pop(0))
        return todo

    before, after = {}, {}
    for k in range(2, UNITS):
        ready = k - 1
        first, second = STEPS[k - 2].split("A")
        before[k] = plan(first)
        assert summed >= k - 2
        ready = k
        after[k] = plan(second)
    ending = plan(LAST + "CC" + "WYWY" + "Y" * UNITS + "Z" * UNITS)

    def carry_out(todo):
        for stage_of, *which in todo:
            stage_of(*which)

    def begin(k):
        if k < 4:
            core_stage(k - 2, 3, 4)
        carry_out(before[k])
        arrive(k)
        for lo, hi in PARTS if k < 4 else ((0, 4),):
            core_copy(k - 2, lo, hi).wait_send()

    def end(k):
        if k == 2:
            dots(1, 1, 3, 4)
            send(1, 3, 4)
        carry_out(after[k])

    def unit(u, carry):
        matrix = ((u + 1) // 3 + 1 + u // 15) % 2
        for k in range(2, UNITS):
            pl.when(u == k)(functools.partial(begin, k))
        queries(u, 0)
        dots(u, matrix, 0, 4)
        send(u, 0, 4)
        for k in range(2, UNITS):
            pl.when(u == k)(functools.partial(end, k))
        return carry

    lax.fori_loop(2, UNITS, unit, 0)
    last = UNITS - 1
    carry_out(ending)

    def gram(u):
        if u in ACROSS_FIRST:
            return csum[u, 3, zl]
        z_copy(u).wait_recv()
        return csum[u, 3, zl] + zin[u]

    def store(dx, flip, value):
        source = ((zh + flip) % 2) * 4 + (x + dx) % 4
        out[:, pl.ds(pl.multiple_of(source * 128, 128), 128)] = value

    def finish(block):
        first, second, dx, flip = block
        store(dx, flip, gram(first) * gram(second))

    halves = gram(2) * gram(5), gram(3) * gram(6)
    store(3, 0, jnp.concatenate([half[:, :64] for half in halves], axis=1))
    store(1, 0, jnp.concatenate([half[:, 64:] for half in halves], axis=1))
    for block in sorted(BLOCKS, key=lambda block: max(done.index(u) for u in block[:2])):
        finish(block)

    for u in (last - 1, last):
        core_copy(u, 0, 4).wait_send()
    whole = pl.ds(0, UNITS - len(ACROSS_FIRST) // 2)
    for ref, sem in ((qbuf.at[pl.ds(2, UNITS - 2)], ag_send), (y1.at[whole], y1_send), (y2.at[whole], y2_send),
                     (zin.at[pl.ds(0, UNITS - len(ACROSS_FIRST))], z_send), (zfirst, first_send)):
        remote(ref, ref, sem, sem, right).wait_send()


def per_device(resident_x, resident_g, query_x, query_g):
    dma = pltpu.SemaphoreType.DMA
    return pl.pallas_call(
        kernel,
        out_shape=jax.ShapeDtypeStruct((128, 1024), F32),
        in_specs=[pl.BlockSpec(memory_space=pl.ANY)] * 4,
        out_specs=pl.BlockSpec(memory_space=pltpu.VMEM),
        scratch_shapes=[
            pltpu.VMEM((2, 4, 512, 1024), BF16),
            pltpu.VMEM((2, 4, 512, 1024), BF16),
            pltpu.VMEM((UNITS, 128, 1024), F32),
            pltpu.VMEM((2, 256, 1024), BF16),
            pltpu.VMEM((STAGES, 256, 1024), F32),
            pltpu.VMEM((2, 2, 4, 2, 128, 128), F32),
            pltpu.VMEM((UNITS, 4, 2, 128, 128), F32),
            pltpu.VMEM((UNITS, 2, 128, 128), F32),
            pltpu.VMEM((UNITS, 2, 2, 128, 128), F32),
            pltpu.VMEM((UNITS, 128, 128), F32),
            pltpu.VMEM((len(ACROSS_FIRST), 4, 128, 128), F32),
            dma((2,)), dma((STAGES,)), dma, dma((UNITS,)), dma((2, 3)), dma((UNITS + 4,)),
            dma, dma((UNITS,)), dma, dma((UNITS,)), dma, dma((UNITS,)), dma, dma((len(ACROSS_FIRST),)),
        ],
        compiler_params=pltpu.CompilerParams(collective_id=0, has_side_effects=True, vmem_limit_bytes=61 * 2**20),
    )(resident_x, resident_g, query_x, query_g)


def solution(mesh):
    return jax.shard_map(
        per_device,
        mesh=mesh,
        in_specs=(P("tok", "wid"), P("tok", "wid"), P("tok", "wid"), P("tok", "wid")),
        out_specs=P(("tok", "wid"), None),
        check_vma=False,
    )
```

```python
import functools

import jax
import jax.numpy as jnp
from jax import lax
from jax.experimental import pallas as pl
from jax.experimental.pallas import tpu as pltpu
from jax.sharding import PartitionSpec as P

MESH = pl.DeviceIdType.MESH
F32, BF16 = jnp.float32, jnp.bfloat16
NT = (((1,), (1,)), ((), ()))

BLOCKS = ((0, 1, 0, 0), (4, 7, 0, 1), (8, 11, 2, 0), (9, 12, 3, 1), (10, 13, 1, 1), (14, 15, 2, 1))
ACROSS_FIRST = (11, 13)
STEPS = ("CyAY", "ACyZW", "yACy", "ACZW", "yACyZ", "ACyW", "ACYCZZZ", "YCAYW", "YAYW", "CyAyC", "AyC", "ACY", "ACYZ", "yAyC")
LAST = "ZCWYWZZYZYZYZZZZZ"
UNITS = 16
REL = (2, 1, 3, 0)
STAGES = 14
PARTS = ((0, 1), (1, 3), (3, 4))


def kernel(rx, rg, qx, qg, out_x, out_g, rh, rl, qbuf, qcat, stage, pbuf, csum, y1, y2, zin, zfirst,
           load_sem, stage_sem, ag_send, ag_recv, c_send, c_recv, y1_send, y1_recv, y2_send, y2_recv, z_send, z_recv, first_send, first_recv):
    t, w = lax.axis_index("tok"), lax.axis_index("wid")
    zh, x = t // 4, t % 4
    zl, y, c = w // 8, (w // 2) % 4, w % 2
    right, left = (zh * 4 + (x + 1) % 4, w), (zh * 4 + (x + 3) % 4, w)
    partner = ((1 - zh) * 4 + x, w)
    up, down = (t, zl * 8 + ((y + 1) % 4) * 2 + c), (t, zl * 8 + ((y + 3) % 4) * 2 + c)
    sibling = (t, zl * 8 + y * 2 + 1 - c)
    across = (t, (1 - zl) * 8 + y * 2 + c)

    def remote(src, dst, send, recv, target):
        return pltpu.make_async_remote_copy(src_ref=src, dst_ref=dst, send_sem=send, recv_sem=recv, device_id=target, device_id_type=MESH)

    def gather(src, start, unit, row, rows, target):
        ref = {0: qx, 1: qg}.get(src, qbuf.at[src])
        return remote(ref.at[pl.ds(start, rows)], qbuf.at[unit, pl.ds(row, rows)], ag_send, ag_recv.at[unit], target)

    own = []
    for m in range(2):
        own += [gather(m, 0, 2 + 3 * m, 0, 64, right), gather(m, 0, 2 + 3 * m, 64, 64, left), gather(m, 0, 4 + 3 * m, 0, 128, partner),
                gather(m, 64, 3 + 3 * m, 0, 64, right), gather(m, 64, 3 + 3 * m, 64, 64, left)]
    forward = {
        2: [gather(2, 0, 8, 0, 64, right)],
        3: [gather(3, 64, 8, 64, 64, left)],
        4: [gather(4, 0, 9, 0, 128, right), gather(4, 0, 10, 0, 128, left)],
        5: [gather(5, 0, 12, 0, 64, partner), gather(5, 64, 13, 0, 64, partner), gather(5, 0, 11, 0, 64, right)],
        6: [gather(6, 0, 12, 64, 64, partner), gather(6, 64, 13, 64, 64, partner), gather(6, 64, 11, 64, 64, left)],
        9: [gather(9, 0, 14, 0, 64, right)],
        10: [gather(10, 64, 14, 64, 64, left)],
        12: [gather(12, 0, 15, 0, 64, right)],
        13: [gather(13, 64, 15, 64, 64, left)],
    }

    def load(matrix, s, half):
        row = pl.multiple_of(half * 1024 + ((y + REL[s]) % 4) * 256, 256)
        slot = (matrix * 8 + s * 2 + half) % STAGES
        return pltpu.make_async_copy((rx, rg)[matrix].at[pl.ds(row, 256)], stage.at[slot], stage_sem.at[slot])

    def split(matrix, *parts):
        for s in parts:
            for half in range(2):
                load(matrix, s, half).wait()
        for s in parts:
            for half in range(2):
                value = stage[(matrix * 8 + s * 2 + half) % STAGES]
                hi = value.astype(BF16)
                rh[matrix, s, pl.ds(half * 256, 256)] = hi
                rl[matrix, s, pl.ds(half * 256, 256)] = (value - hi.astype(F32)).astype(BF16)

    barrier = pltpu.get_barrier_semaphore()
    others = (right, left, partner, up, down, sibling, across)
    for other in others:
        pl.semaphore_signal(barrier, inc=1, device_id=other, device_id_type=MESH)
    mine = [pltpu.make_async_copy(qx, qbuf.at[0], load_sem.at[0]), pltpu.make_async_copy(qg, qbuf.at[1], load_sem.at[1])]
    mine[0].start()
    for matrix, s in ((0, 0), (0, 1), (0, 2), (1, 0), (0, 3), (1, 1), (1, 2)):
        for half in range(2):
            load(matrix, s, half).start()
        if (matrix, s) == (0, 0):
            mine[1].start()

    def core_copy(u, lo, hi):
        parts, part = pl.ds(lo, hi - lo), (lo + 1) // 2
        return remote(pbuf.at[u % 2, 1 - c, parts], csum.at[u, parts], c_send.at[u % 2, part], c_recv.at[UNITS + 2 * u + part - 1 if part else u], sibling)

    def y1_copies(u):
        if u in ACROSS_FIRST:
            low, high = pl.ds(0, 64), pl.ds(64, 64)
            return (remote(csum.at[u, 0, zl, low], y1.at[u, 0, low], y1_send, y1_recv.at[u], up),
                    remote(csum.at[u, 0, zl, high], y1.at[u, 1, high], y1_send, y1_recv.at[u], down))
        return (remote(csum.at[u, 0, 0], y1.at[u, 0], y1_send, y1_recv.at[u], up),
                remote(csum.at[u, 0, 1], y1.at[u, 1], y1_send, y1_recv.at[u], down))

    def y2_copies(u):
        if u in ACROSS_FIRST:
            return (remote(csum.at[u, 1, zl], y2.at[u, 0, 0], y2_send, y2_recv.at[u], up),
                    remote(csum.at[u, 2, zl], y2.at[u, 1, 0], y2_send, y2_recv.at[u], down))
        return (remote(csum.at[u, 1], y2.at[u, 0], y2_send, y2_recv.at[u], up),
                remote(csum.at[u, 2], y2.at[u, 1], y2_send, y2_recv.at[u], down))

    def z_copy(u):
        return remote(csum.at[u, 3, 1 - zl], zin.at[u], z_send, z_recv.at[u], across)

    def first_copy(u):
        i = ACROSS_FIRST.index(u)
        return remote(csum.at[u, :, 1 - zl], zfirst.at[i], first_send, first_recv.at[i], across)

    def arrive(k):
        remote(qbuf.at[k], qbuf.at[k], ag_send, ag_recv.at[k], right).wait_recv()
        for copy in forward.get(k, ()):
            copy.start()

    def core_stage(u, lo, hi):
        core_copy(u, lo, hi).wait_recv()
        for s in range(lo, hi):
            csum[u, s] += pbuf[u % 2, c, s]
            if s == 0 and u not in ACROSS_FIRST:
                for copy in y1_copies(u):
                    copy.start()
        if u in ACROSS_FIRST:
            first_copy(u).start()

    def across_stage(u):
        first_copy(u).wait_recv()
        for s in range(4):
            csum[u, s, zl] += zfirst[ACROSS_FIRST.index(u), s]
            if s == 0:
                for copy in y1_copies(u):
                    copy.start()

    def y1_stage(u):
        half = u in ACROSS_FIRST
        landed = y1.at[u, :, pl.ds(0, 64)] if half else y1.at[u]
        remote(landed, landed, y1_send, y1_recv.at[u], up).wait_recv()
        for i, copy in enumerate(y2_copies(u)):
            if half:
                rows = pl.ds(i * 64, 64)
                csum[u, 1 + i, zl, rows] += y1[u, i, rows]
            else:
                csum[u, 1 + i, i] += y1[u, i]
            copy.start()

    def y2_stage(u):
        half = u in ACROSS_FIRST
        landed = y2.at[u, :, 0] if half else y2.at[u]
        remote(landed, landed, y2_send, y2_recv.at[u], up).wait_recv()
        if half:
            csum[u, 3, zl] += y2[u, 0, 0] + y2[u, 1, 0]
        else:
            csum[u, 3] += y2[u, 0] + y2[u, 1]
            z_copy(u).start()

    def queries(u, slot):
        value = qbuf[u]
        hi = value.astype(BF16)
        qcat[slot, pl.ds(0, 128)] = hi
        qcat[slot, pl.ds(128, 128)] = (value - hi.astype(F32)).astype(BF16)

    def dots(u, matrix, lo, hi):
        q = qcat[u if isinstance(u, int) else 0]
        for s in range(lo, hi):
            product = lax.dot_general(rh[matrix, s], q, NT, preferred_element_type=F32)
            product += lax.dot_general(rl[matrix, s], q, NT, preferred_element_type=F32)
            product = product[:, :128] + product[:, 128:]
            for i in range(4):
                pbuf[u % 2, i % 2, s, i // 2] = product[i * 128:(i + 1) * 128]

    def send(u, lo, hi):
        core_copy(u, lo, hi).start()

    mine[0].wait()
    queries(0, 0)
    split(0, 0)
    for half in range(2):
        load(1, 3, half).start()
    dots(0, 0, 0, 1)
    pl.semaphore_wait(barrier, len(others))
    send(0, 0, 1)
    for copy in own:
        copy.start()
    mine[1].wait()
    queries(1, 1)
    split(0, 1, 2)
    split(1, 0)
    core_stage(0, 0, 1)
    dots(1, 1, 0, 1)
    send(1, 0, 1)
    dots(0, 0, 1, 3)
    send(0, 1, 3)
    core_stage(1, 0, 1)
    split(1, 1, 2)
    core_stage(0, 1, 3)
    y1_stage(0)
    dots(1, 1, 1, 3)
    send(1, 1, 3)
    split(0, 3)
    split(1, 3)
    dots(0, 0, 3, 4)
    send(0, 3, 4)
    core_stage(1, 1, 3)
    y1_stage(1)

    summed, on_y1, on_y2, on_z = 1, [], [0, 1], []
    done = []

    def plan(steps):
        nonlocal summed
        todo = []
        for step in steps:
            if step == "C" and summed < ready:
                summed += 1
                todo.append((core_stage, summed, 0, 4))
                (on_z if summed in ACROSS_FIRST else on_y1).append(summed)
            elif step == "W" and on_z:
                todo.append((across_stage, on_z[0]))
                on_y1.append(on_z.pop(0))
            elif step in "Yy" and len(on_y1) > (step == "y"):
                todo.append((y1_stage, on_y1[0]))
                on_y2.append(on_y1.pop(0))
            elif step == "Z" and on_y2:
                todo.append((y2_stage, on_y2[0]))
                done.append(on_y2.pop(0))
        return todo

    before, after = {}, {}
    for k in range(2, UNITS):
        ready = k - 1
        first, second = STEPS[k - 2].split("A")
        before[k] = plan(first)
        assert summed >= k - 2
        ready = k
        after[k] = plan(second)
    ending = plan(LAST + "CC" + "WYWY" + "Y" * UNITS + "Z" * UNITS)

    def carry_out(todo):
        for stage_of, *which in todo:
            stage_of(*which)

    def begin(k):
        if k < 4:
            core_stage(k - 2, 3, 4)
        carry_out(before[k])
        arrive(k)
        for lo, hi in PARTS if k < 4 else ((0, 4),):
            core_copy(k - 2, lo, hi).wait_send()

    def end(k):
        if k == 2:
            dots(1, 1, 3, 4)
            send(1, 3, 4)
        carry_out(after[k])

    def unit(u, carry):
        matrix = ((u + 1) // 3 + 1 + u // 15) % 2
        for k in range(2, UNITS):
            pl.when(u == k)(functools.partial(begin, k))
        queries(u, 0)
        dots(u, matrix, 0, 4)
        send(u, 0, 4)
        for k in range(2, UNITS):
            pl.when(u == k)(functools.partial(end, k))
        return carry

    lax.fori_loop(2, UNITS, unit, 0)
    last = UNITS - 1
    carry_out(ending)

    def gram(u):
        if u in ACROSS_FIRST:
            return csum[u, 3, zl]
        z_copy(u).wait_recv()
        return csum[u, 3, zl] + zin[u]

    def store(out, dx, flip, value):
        source = ((zh + flip) % 2) * 4 + (x + dx) % 4
        out[:, pl.ds(pl.multiple_of(source * 128, 128), 128)] = value

    for out, first, second in ((out_x, 2, 3), (out_g, 5, 6)):
        halves = gram(first), gram(second)
        store(out, 3, 0, jnp.concatenate([half[:, :64] for half in halves], axis=1))
        store(out, 1, 0, jnp.concatenate([half[:, 64:] for half in halves], axis=1))
    places = {u: (out, dx, flip) for *units, dx, flip in BLOCKS for u, out in zip(units, (out_x, out_g))}
    for u in sorted(places, key=done.index):
        store(*places[u], gram(u))

    for u in (last - 1, last):
        core_copy(u, 0, 4).wait_send()
    whole = pl.ds(0, UNITS - len(ACROSS_FIRST) // 2)
    for ref, sem in ((qbuf.at[pl.ds(2, UNITS - 2)], ag_send), (y1.at[whole], y1_send), (y2.at[whole], y2_send),
                     (zin.at[pl.ds(0, UNITS - len(ACROSS_FIRST))], z_send), (zfirst, first_send)):
        remote(ref, ref, sem, sem, right).wait_send()


def per_device(resident_x, resident_g, query_x, query_g):
    dma = pltpu.SemaphoreType.DMA
    input_gram, grad_gram = pl.pallas_call(
        kernel,
        out_shape=[jax.ShapeDtypeStruct((128, 1024), F32)] * 2,
        in_specs=[pl.BlockSpec(memory_space=pl.ANY)] * 4,
        out_specs=[pl.BlockSpec(memory_space=pltpu.VMEM)] * 2,
        scratch_shapes=[
            pltpu.VMEM((2, 4, 512, 1024), BF16),
            pltpu.VMEM((2, 4, 512, 1024), BF16),
            pltpu.VMEM((UNITS, 128, 1024), F32),
            pltpu.VMEM((2, 256, 1024), BF16),
            pltpu.VMEM((STAGES, 256, 1024), F32),
            pltpu.VMEM((2, 2, 4, 2, 128, 128), F32),
            pltpu.VMEM((UNITS, 4, 2, 128, 128), F32),
            pltpu.VMEM((UNITS, 2, 128, 128), F32),
            pltpu.VMEM((UNITS, 2, 2, 128, 128), F32),
            pltpu.VMEM((UNITS, 128, 128), F32),
            pltpu.VMEM((len(ACROSS_FIRST), 4, 128, 128), F32),
            dma((2,)), dma((STAGES,)), dma, dma((UNITS,)), dma((2, 3)), dma((UNITS + 4,)),
            dma, dma((UNITS,)), dma, dma((UNITS,)), dma, dma((UNITS,)), dma, dma((len(ACROSS_FIRST),)),
        ],
        compiler_params=pltpu.CompilerParams(collective_id=0, has_side_effects=True, vmem_limit_bytes=61 * 2**20),
    )(resident_x, resident_g, query_x, query_g)
    return input_gram * grad_gram


def solution(mesh):
    return jax.shard_map(
        per_device,
        mesh=mesh,
        in_specs=(P("tok", "wid"), P("tok", "wid"), P("tok", "wid"), P("tok", "wid")),
        out_specs=P(("tok", "wid"), None),
        check_vma=False,
    )
```

```python
import functools

import jax
import jax.numpy as jnp
from jax import lax
from jax.experimental import pallas as pl
from jax.experimental.pallas import tpu as pltpu
from jax.sharding import PartitionSpec as P

MESH = pl.DeviceIdType.MESH
F32, BF16 = jnp.float32, jnp.bfloat16
NT = (((1,), (1,)), ((), ()))

BLOCKS = ((0, 1, 0, 0), (4, 7, 0, 1), (8, 11, 2, 0), (9, 12, 3, 1), (10, 13, 1, 1), (14, 15, 2, 1))
ACROSS_FIRST = (11, 13)
STEPS = ("Ay", "Ay", "yCACYZ", "AC", "A", "YCACYCZ", "CyACYZZZW", "CyAy", "ACW", "YAyCZ", "AyC", "Ay", "CYACY", "ACy")
LAST = "CWZZYZZWZYZZYYZZZZZZ"
UNITS = 16
REL = (2, 1, 3, 0)
STAGES = 14
PARTS = ((0, 1), (1, 3), (3, 4))


def kernel(rx, rg, qx, qg, out_x, out_g, rh, rl, qbuf, qcat, stage, pbuf, csum, y1, y2, zin, zfirst,
           load_sem, stage_sem, ag_send, ag_recv, c_send, c_recv, y1_send, y1_recv, y2_send, y2_recv, z_send, z_recv, first_send, first_recv):
    t, w = lax.axis_index("tok"), lax.axis_index("wid")
    zh, x = t // 4, t % 4
    zl, y, c = w // 8, (w // 2) % 4, w % 2
    right, left = (zh * 4 + (x + 1) % 4, w), (zh * 4 + (x + 3) % 4, w)
    partner = ((1 - zh) * 4 + x, w)
    up, down = (t, zl * 8 + ((y + 1) % 4) * 2 + c), (t, zl * 8 + ((y + 3) % 4) * 2 + c)
    sibling = (t, zl * 8 + y * 2 + 1 - c)
    across = (t, (1 - zl) * 8 + y * 2 + c)

    def remote(src, dst, send, recv, target):
        return pltpu.make_async_remote_copy(src_ref=src, dst_ref=dst, send_sem=send, recv_sem=recv, device_id=target, device_id_type=MESH)

    def gather(src, start, unit, row, rows, target):
        ref = {0: qx, 1: qg}.get(src, qbuf.at[src])
        return remote(ref.at[pl.ds(start, rows)], qbuf.at[unit, pl.ds(row, rows)], ag_send, ag_recv.at[unit], target)

    own = []
    for m in range(2):
        own += [gather(m, 0, 2 + 3 * m, 0, 64, right), gather(m, 0, 2 + 3 * m, 64, 64, left), gather(m, 0, 4 + 3 * m, 0, 128, partner),
                gather(m, 64, 3 + 3 * m, 0, 64, right), gather(m, 64, 3 + 3 * m, 64, 64, left)]
    forward = {
        2: [gather(2, 0, 8, 0, 64, right)],
        3: [gather(3, 64, 8, 64, 64, left)],
        4: [gather(4, 0, 9, 0, 128, right), gather(4, 0, 10, 0, 128, left)],
        5: [gather(5, 0, 12, 0, 64, partner), gather(5, 64, 13, 0, 64, partner), gather(5, 0, 11, 0, 64, right)],
        6: [gather(6, 0, 12, 64, 64, partner), gather(6, 64, 13, 64, 64, partner), gather(6, 64, 11, 64, 64, left)],
        9: [gather(9, 0, 14, 0, 64, right)],
        10: [gather(10, 64, 14, 64, 64, left)],
        12: [gather(12, 0, 15, 0, 64, right)],
        13: [gather(13, 64, 15, 64, 64, left)],
    }

    def load(matrix, s, half):
        row = pl.multiple_of(half * 1024 + ((y + REL[s]) % 4) * 256, 256)
        slot = (matrix * 8 + s * 2 + half) % STAGES
        return pltpu.make_async_copy((rx, rg)[matrix].at[pl.ds(row, 256)], stage.at[slot], stage_sem.at[slot])

    def split(matrix, *parts):
        for s in parts:
            for half in range(2):
                load(matrix, s, half).wait()
        for s in parts:
            for half in range(2):
                value = stage[(matrix * 8 + s * 2 + half) % STAGES]
                hi = value.astype(BF16)
                rh[matrix, s, pl.ds(half * 256, 256)] = hi
                rl[matrix, s, pl.ds(half * 256, 256)] = (value - hi.astype(F32)).astype(BF16)

    barrier = pltpu.get_barrier_semaphore()
    others = (right, left, partner, up, down, sibling, across)
    for other in others:
        pl.semaphore_signal(barrier, inc=1, device_id=other, device_id_type=MESH)
    mine = [pltpu.make_async_copy(qx, qbuf.at[0], load_sem.at[0]), pltpu.make_async_copy(qg, qbuf.at[1], load_sem.at[1])]
    mine[0].start()
    for matrix, s in ((0, 0), (0, 1), (0, 2), (1, 0), (0, 3), (1, 1), (1, 2)):
        for half in range(2):
            load(matrix, s, half).start()
        if (matrix, s) == (0, 0):
            mine[1].start()

    def core_copy(u, lo, hi):
        parts, part = pl.ds(lo, hi - lo), (lo + 1) // 2
        return remote(pbuf.at[u % 2, 1 - c, parts], csum.at[u, parts], c_send.at[u % 2, part], c_recv.at[UNITS + 2 * u + part - 1 if part else u], sibling)

    def y1_copies(u):
        if u in ACROSS_FIRST:
            low, high = pl.ds(0, 64), pl.ds(64, 64)
            return (remote(csum.at[u, 0, zl, low], y1.at[u, 0, low], y1_send, y1_recv.at[u], up),
                    remote(csum.at[u, 0, zl, high], y1.at[u, 1, high], y1_send, y1_recv.at[u], down))
        return (remote(csum.at[u, 0, 0], y1.at[u, 0], y1_send, y1_recv.at[u], up),
                remote(csum.at[u, 0, 1], y1.at[u, 1], y1_send, y1_recv.at[u], down))

    def y2_copies(u):
        if u in ACROSS_FIRST:
            return (remote(csum.at[u, 1, zl], y2.at[u, 0, 0], y2_send, y2_recv.at[u], up),
                    remote(csum.at[u, 2, zl], y2.at[u, 1, 0], y2_send, y2_recv.at[u], down))
        return (remote(csum.at[u, 1], y2.at[u, 0], y2_send, y2_recv.at[u], up),
                remote(csum.at[u, 2], y2.at[u, 1], y2_send, y2_recv.at[u], down))

    def z_copy(u):
        return remote(csum.at[u, 3, 1 - zl], zin.at[u], z_send, z_recv.at[u], across)

    def first_copy(u):
        i = ACROSS_FIRST.index(u)
        return remote(csum.at[u, :, 1 - zl], zfirst.at[i], first_send, first_recv.at[i], across)

    def arrive(k):
        remote(qbuf.at[k], qbuf.at[k], ag_send, ag_recv.at[k], right).wait_recv()
        for copy in forward.get(k, ()):
            copy.start()

    def core_stage(u, lo, hi):
        core_copy(u, lo, hi).wait_recv()
        for s in range(lo, hi):
            csum[u, s] += pbuf[u % 2, c, s]
            if s == 0 and u not in ACROSS_FIRST:
                for copy in y1_copies(u):
                    copy.start()
        if u in ACROSS_FIRST:
            first_copy(u).start()

    def across_stage(u):
        first_copy(u).wait_recv()
        for s in range(4):
            csum[u, s, zl] += zfirst[ACROSS_FIRST.index(u), s]
            if s == 0:
                for copy in y1_copies(u):
                    copy.start()

    def y1_stage(u):
        half = u in ACROSS_FIRST
        landed = y1.at[u, :, pl.ds(0, 64)] if half else y1.at[u]
        remote(landed, landed, y1_send, y1_recv.at[u], up).wait_recv()
        for i, copy in enumerate(y2_copies(u)):
            if half:
                rows = pl.ds(i * 64, 64)
                csum[u, 1 + i, zl, rows] += y1[u, i, rows]
            else:
                csum[u, 1 + i, i] += y1[u, i]
            copy.start()

    def y2_stage(u):
        half = u in ACROSS_FIRST
        landed = y2.at[u, :, 0] if half else y2.at[u]
        remote(landed, landed, y2_send, y2_recv.at[u], up).wait_recv()
        if half:
            csum[u, 3, zl] += y2[u, 0, 0] + y2[u, 1, 0]
        else:
            csum[u, 3] += y2[u, 0] + y2[u, 1]
            z_copy(u).start()

    def queries(u, slot):
        value = qbuf[u]
        hi = value.astype(BF16)
        qcat[slot, pl.ds(0, 128)] = hi
        qcat[slot, pl.ds(128, 128)] = (value - hi.astype(F32)).astype(BF16)

    def dots(u, matrix, lo, hi):
        q = qcat[u if isinstance(u, int) else 0]
        for s in range(lo, hi):
            product = lax.dot_general(rh[matrix, s], q, NT, preferred_element_type=F32)
            product += lax.dot_general(rl[matrix, s], q, NT, preferred_element_type=F32)
            product = product[:, :128] + product[:, 128:]
            for i in range(4):
                pbuf[u % 2, i % 2, s, i // 2] = product[i * 128:(i + 1) * 128]

    def send(u, lo, hi):
        core_copy(u, lo, hi).start()

    mine[0].wait()
    queries(0, 0)
    split(0, 0)
    for half in range(2):
        load(1, 3, half).start()
    dots(0, 0, 0, 1)
    pl.semaphore_wait(barrier, len(others))
    send(0, 0, 1)
    for copy in own:
        copy.start()
    mine[1].wait()
    queries(1, 1)
    split(0, 1, 2)
    split(1, 0)
    core_stage(0, 0, 1)
    dots(1, 1, 0, 1)
    send(1, 0, 1)
    dots(0, 0, 1, 3)
    send(0, 1, 3)
    core_stage(1, 0, 1)
    split(1, 1, 2)
    core_stage(0, 1, 3)
    y1_stage(0)
    dots(1, 1, 1, 3)
    send(1, 1, 3)
    split(0, 3)
    split(1, 3)
    dots(0, 0, 3, 4)
    send(0, 3, 4)
    core_stage(1, 1, 3)
    y1_stage(1)

    summed, on_y1, on_y2, on_z = 1, [], [0, 1], []
    done = []

    def plan(steps):
        nonlocal summed
        todo = []
        for step in steps:
            if step == "C" and summed < ready:
                summed += 1
                todo.append((core_stage, summed, 0, 4))
                (on_z if summed in ACROSS_FIRST else on_y1).append(summed)
            elif step == "W" and on_z:
                todo.append((across_stage, on_z[0]))
                on_y1.append(on_z.pop(0))
            elif step in "Yy" and len(on_y1) > (step == "y"):
                todo.append((y1_stage, on_y1[0]))
                on_y2.append(on_y1.pop(0))
            elif step == "Z" and on_y2:
                todo.append((y2_stage, on_y2[0]))
                done.append(on_y2.pop(0))
        return todo

    before, after = {}, {}
    for k in range(2, UNITS):
        ready = k - 1
        first, second = STEPS[k - 2].split("A")
        before[k] = plan(first)
        assert summed >= k - 2
        ready = k
        after[k] = plan(second)
    ending = plan(LAST + "CC" + "WYWY" + "Y" * UNITS + "Z" * UNITS)

    def carry_out(todo):
        for stage_of, *which in todo:
            stage_of(*which)

    def begin(k):
        if k < 4:
            core_stage(k - 2, 3, 4)
        carry_out(before[k])
        arrive(k)
        for lo, hi in PARTS if k < 4 else ((0, 4),):
            core_copy(k - 2, lo, hi).wait_send()

    def end(k):
        if k == 2:
            dots(1, 1, 3, 4)
            send(1, 3, 4)
        carry_out(after[k])

    def unit(u, carry):
        matrix = ((u + 1) // 3 + 1 + u // 15) % 2
        for k in range(2, UNITS):
            pl.when(u == k)(functools.partial(begin, k))
        queries(u, 0)
        dots(u, matrix, 0, 4)
        send(u, 0, 4)
        for k in range(2, UNITS):
            pl.when(u == k)(functools.partial(end, k))
        return carry

    lax.fori_loop(2, UNITS, unit, 0)
    last = UNITS - 1
    carry_out(ending)

    def gram(u):
        if u in ACROSS_FIRST:
            return csum[u, 3, zl]
        z_copy(u).wait_recv()
        return csum[u, 3, zl] + zin[u]

    def store(out, dx, flip, value):
        source = ((zh + flip) % 2) * 4 + (x + dx) % 4
        out[:, pl.ds(pl.multiple_of(source * 128, 128), 128)] = value

    for out, first, second in ((out_x, 2, 3), (out_g, 5, 6)):
        halves = gram(first), gram(second)
        store(out, 3, 0, jnp.concatenate([half[:, :64] for half in halves], axis=1))
        store(out, 1, 0, jnp.concatenate([half[:, 64:] for half in halves], axis=1))
    places = {u: (out, dx, flip) for *units, dx, flip in BLOCKS for u, out in zip(units, (out_x, out_g))}
    for u in sorted(places, key=done.index):
        store(*places[u], gram(u))

    for u in (last - 1, last):
        core_copy(u, 0, 4).wait_send()
    whole = pl.ds(0, UNITS - len(ACROSS_FIRST) // 2)
    for ref, sem in ((qbuf.at[pl.ds(2, UNITS - 2)], ag_send), (y1.at[whole], y1_send), (y2.at[whole], y2_send),
                     (zin.at[pl.ds(0, UNITS - len(ACROSS_FIRST))], z_send), (zfirst, first_send)):
        remote(ref, ref, sem, sem, right).wait_send()


def per_device(resident_x, resident_g, query_x, query_g):
    dma = pltpu.SemaphoreType.DMA
    input_gram, grad_gram = pl.pallas_call(
        kernel,
        out_shape=[jax.ShapeDtypeStruct((128, 1024), F32)] * 2,
        in_specs=[pl.BlockSpec(memory_space=pl.ANY)] * 4,
        out_specs=[pl.BlockSpec(memory_space=pltpu.VMEM)] * 2,
        scratch_shapes=[
            pltpu.VMEM((2, 4, 512, 1024), BF16),
            pltpu.VMEM((2, 4, 512, 1024), BF16),
            pltpu.VMEM((UNITS, 128, 1024), F32),
            pltpu.VMEM((2, 256, 1024), BF16),
            pltpu.VMEM((STAGES, 256, 1024), F32),
            pltpu.VMEM((2, 2, 4, 2, 128, 128), F32),
            pltpu.VMEM((UNITS, 4, 2, 128, 128), F32),
            pltpu.VMEM((UNITS, 2, 128, 128), F32),
            pltpu.VMEM((UNITS, 2, 2, 128, 128), F32),
            pltpu.VMEM((UNITS, 128, 128), F32),
            pltpu.VMEM((len(ACROSS_FIRST), 4, 128, 128), F32),
            dma((2,)), dma((STAGES,)), dma, dma((UNITS,)), dma((2, 3)), dma((UNITS + 4,)),
            dma, dma((UNITS,)), dma, dma((UNITS,)), dma, dma((UNITS,)), dma, dma((len(ACROSS_FIRST),)),
        ],
        compiler_params=pltpu.CompilerParams(collective_id=0, has_side_effects=True, vmem_limit_bytes=61 * 2**20),
    )(resident_x, resident_g, query_x, query_g)
    return input_gram * grad_gram


def solution(mesh):
    return jax.shard_map(
        per_device,
        mesh=mesh,
        in_specs=(P("tok", "wid"), P("tok", "wid"), P("tok", "wid"), P("tok", "wid")),
        out_specs=P(("tok", "wid"), None),
        check_vma=False,
    )
```
